512 devices in a mesh: blk: 32 (over x, y, z_hi), rep: 16 (over z_lo, core).
Axes of the slice: x: 4, y: 4, z: 16 (z_hi: 2, z_lo: 8; z = z_hi * 8 + z_lo), core: 2. Of those that a mesh axis runs over, the one named last changes fastest.
Arguments:
- coords: float32 [192, 65536], P('rep', 'blk'), may hold values from -4 to 4
- eigvecs: float32 [128, 65536], P(None, ('blk', 'rep')), may hold values from -0.36 to 0.36
- nbr_list: int32 [512, 128], P('blk'), may hold values from 0 to 511, as said below
- nbr_count: int32 [512], P('blk'), may hold values from 32 to 128, as said below
Outputs:
- smoothed: float32 [128, 65536], P(None, ('blk', 'rep'))
The draws below stay inside these ranges and needn't reach their ends.
Inputs may be any that keep to these rules, and one draw needn't show every extreme that they name: `nbr_count`: the largest count is exactly 128 in every draw; counts differ from block to block. `nbr_list`: the first nbr_count entries of a row are distinct block indices; entries after them are not used.
All inputs are finite; a program needn't handle non-finite values.
Results may differ from the reference program's by a relative error of at most 0.0003.
Values sent between devices are 32-bit elements; how exact they have to be, the bound alone decides.
A program may use at most 64 MiB of HBM per device.

```python
import jax
import jax.numpy as jnp
from jax import lax

TRAJ_BLOCK = 128
T_SAMPLES = 64
COORDS = 3
EIG = 128
FEAT = 192
NBLOCKS = 512
NTRAJ = 65536
NBR_MAX = 128
NBR_MIN = 32


def draw_coords(key, part):
    start_key, speed_key, accel_key, noise_key = jax.random.split(jax.random.fold_in(key, 3), 4)
    times = jnp.arange(T_SAMPLES, dtype=jnp.float32) / T_SAMPLES
    start = jax.random.uniform(start_key, (COORDS, 1, NTRAJ), jnp.float32, -1.0, 1.0)
    speed = 0.4 * jnp.clip(jax.random.normal(speed_key, (COORDS, 1, NTRAJ), jnp.float32), -2.0, 2.0)
    accel = 0.3 * jnp.clip(jax.random.normal(accel_key, (COORDS, 1, NTRAJ), jnp.float32), -2.0, 2.0)
    noise = 0.25 * jnp.clip(jax.random.normal(noise_key, (COORDS, T_SAMPLES, NTRAJ), jnp.float32), -4.0, 4.0)
    values = start + speed * times[None, :, None] + accel * (times * times)[None, :, None] + noise
    return values.reshape(FEAT, NTRAJ)


def draw_nbr_count(key, part):
    base_key, factor_key, peak_key = jax.random.split(jax.random.fold_in(key, 7), 3)
    spread = jax.random.randint(base_key, (NBLOCKS,), 0, NBR_MAX - NBR_MIN + 1)
    factor = jax.random.randint(factor_key, (NBLOCKS,), 1, 5)
    counts = NBR_MIN + spread * factor // 4
    peak = jax.random.randint(peak_key, (), 0, NBLOCKS)
    return jnp.where(jnp.arange(NBLOCKS, dtype=jnp.int32) == peak, NBR_MAX, counts).astype(jnp.int32)


def draw_nbr_list(key, part):
    score_key = jax.random.fold_in(key, 11)
    scores = jax.random.randint(score_key, (NBLOCKS, NBLOCKS), 0, 262144) * NBLOCKS
    scores = scores + jnp.arange(NBLOCKS, dtype=jnp.int32)[None, :]
    picked = lax.top_k(scores, NBR_MAX)[1]
    return picked.astype(jnp.int32)


def block_scale(stream_key, extent, pieces, low, high):
    loudness, own = 1.0, jax.random.fold_in(stream_key, 6)
    for axis_at, shards_of in pieces:
        heights = jnp.exp(jax.random.uniform(jax.random.fold_in(own, axis_at), (shards_of,), jnp.float32, low / len(pieces), high / len(pieces)))
        loudness = loudness * jnp.repeat(heights, extent[axis_at] // shards_of).reshape([-1 if axis == axis_at else 1 for axis in range(len(extent))])
    return loudness


def gaussian(own_key, shape, scale, bound, cuts=(), kind=jnp.bfloat16):
    level = block_scale(own_key, shape, cuts, -0.22, 0.18) if cuts else 1.0
    array = jax.random.normal(own_key, shape, jnp.float32) * scale * level
    return jnp.minimum(jnp.maximum(array, -bound), bound).astype(kind)


def setup_inputs(seed: int = 0) -> dict:
    keys = jax.random.split(jax.random.key(seed), 5)
    coords = draw_coords(jax.random.fold_in(keys[4], 71), 0)
    eigvecs = gaussian(keys[1], (EIG, NTRAJ), 0.06, 0.36, ((1, 512),), jnp.float32)
    nbr_list = draw_nbr_list(jax.random.fold_in(keys[4], 71), 0)
    nbr_count = draw_nbr_count(jax.random.fold_in(keys[4], 71), 0)
    return dict(coords=coords, eigvecs=eigvecs, nbr_list=nbr_list, nbr_count=nbr_count)


def reference(coords, eigvecs, nbr_list, nbr_count):
    tiles = coords.reshape(FEAT, NBLOCKS, TRAJ_BLOCK)
    vec_tiles = eigvecs.reshape(EIG, NBLOCKS, TRAJ_BLOCK)
    norms = jnp.sum(tiles * tiles, axis=0)
    slot_ids = jnp.arange(NBR_MAX, dtype=jnp.int32)
    kernel_scale = FEAT * 1.0

    def one_block(inputs):
        row_id, neighbours, count = inputs
        row_x = jnp.take(tiles, row_id, axis=1)
        col_x = jnp.take(tiles, neighbours, axis=1)
        col_v = jnp.take(vec_tiles, neighbours, axis=1)
        inner_prod = jnp.einsum("ft,fku->ktu", row_x, col_x, precision=lax.Precision.HIGHEST)
        row_sq = jnp.take(norms, row_id, axis=0)
        col_sq = jnp.take(norms, neighbours, axis=0)
        dist_sq = row_sq[None, :, None] + col_sq[:, None, :] - 2.0 * inner_prod
        weight = jnp.exp(-dist_sq / kernel_scale)
        weight = jnp.where((slot_ids < count)[:, None, None], weight, 0.0)
        return jnp.einsum("ktu,eku->et", weight, col_v, precision=lax.Precision.HIGHEST)

    blocks = lax.map(one_block, (jnp.arange(NBLOCKS, dtype=jnp.int32), nbr_list, nbr_count))
    return jnp.transpose(blocks, (1, 0, 2)).reshape(EIG, NTRAJ)
```

```python
import functools
import math

import jax
import jax.numpy as jnp
from jax import lax
from jax.experimental import pallas as pl
from jax.experimental.pallas import tpu as pltpu
from jax.sharding import PartitionSpec as P

MESH = pl.DeviceIdType.MESH
X, Y, Z = 4, 4, 16
HALF = Z // 2
PLANE = X * Y
FEAT, EIG, BLOCK = 192, 128, 128
PANEL = FEAT + EIG
PART = 12
PART_PAD = 16
REP = 16
ROOT = math.sqrt(2.0 * math.log2(math.e) / FEAT)


def rem(a, b):
    return lax.rem(a, jnp.int32(b))


def place():
    blk, rep = lax.axis_index("blk"), lax.axis_index("rep")
    core, zl = rem(rep, 2), rep // 2
    zh, xy = rem(blk, 2), blk // 2
    return blk, rep, core, xy // Y, rem(xy, Y), zh * HALF + zl


def device(x, y, z, core):
    return {"blk": (x * Y + y) * 2 + z // HALF, "rep": rem(z, HALF) * 2 + core}


def copy_to(src, dst, send, recv, where):
    return pltpu.make_async_remote_copy(
        src_ref=src, dst_ref=dst, send_sem=send, recv_sem=recv, device_id=where, device_id_type=MESH
    )


def scale_of(x):
    return jnp.exp2(-0.5 * jnp.sum(x * x, axis=0, keepdims=True))


def gather_kernel(
    parts, vecs, lists, rows, cols, far_lists, own_scale, landed,
    part_send, part_recv, list_send, list_recv, z_send, z_recv, xy_send, xy_recv, pair_send, pair_recv,
):
    blk, rep, core, x, y, z = place()
    other = 1 - core
    here = device(x, y, z, core)
    up, down = rem(z + 1, Z), rem(z + Z - 1, Z)
    far = rem(z + HALF, Z)

    barrier = pltpu.get_barrier_semaphore()
    mates = [{"blk": blk, "rep": rem(rep + d, REP)} for d in range(1, REP)]
    mates += [device(x, y, up, core), device(x, y, down, core), device(x, y, far, core)]
    mates += [device(rem(x + d, X), y, z, core) for d in (1, X - 1)]
    mates += [device(x, rem(y + d, Y), z, core) for d in (1, Y - 1)]
    for mate in mates:
        pl.semaphore_signal(barrier, inc=1, device_id=mate, device_id_type=MESH)
    pl.semaphore_wait(barrier, len(mates))

    for d in range(1, REP):
        to = rem(rep + d, REP)
        copy_to(parts.at[to], landed.at[rep], part_send, part_recv, {"blk": blk, "rep": to}).start()
    cols[x * Y + y, core, FEAT:] = vecs[...]
    landed[rep] = parts[rep]
    copy_to(lists, far_lists, list_send, list_recv, device(x, y, far, core)).start()

    def plane_steps(phase, base, size):
        half, quarter = size // 2, size // 4

        def spot(turn, i, j):
            dx, dy = (i, j) if turn == 0 else (j, i)
            return rem(x + dx + X, X), rem(y + dy + Y, Y)

        def region(turn, i, j, part):
            sx, sy = spot(turn, i, j)
            start, count = base + turn * half, half
            if part is not None:
                start, count = start + part * quarter, quarter
            return cols.at[sx * Y + sy, core, pl.ds(start, count)]

        def send(turn, slot, i, j, part, to):
            tx, ty = spot(turn, *to)
            ref = region(turn, i, j, part)
            src = vecs.at[pl.ds(turn * half, half)] if phase == 0 and (i, j) == (0, 0) else ref
            copy_to(src, ref, xy_send, xy_recv.at[phase, turn * 20 + slot], device(tx, ty, z, core)).start()

        def arrive(turn, slot, i, j, part):
            ref = region(turn, i, j, part)
            copy_to(ref, ref, xy_send, xy_recv.at[phase, turn * 20 + slot], here).wait_recv()

        def share(turn, i, j):
            ref = region(turn, i, j, None)
            src = vecs.at[pl.ds(turn * half, half)] if phase == 0 and (i, j) == (0, 0) else ref
            copy_to(src, ref, pair_send, pair_recv, device(x, y, z, other)).start()

        def spread(n, i):
            for turn in range(2):
                send(turn, 4 + 4 * n, i, 0, None, (0, 1))
                send(turn, 5 + 4 * n, i, 0, None, (0, -1))

        def relay(n, i):
            for turn in range(2):
                arrive(turn, 4 + 4 * n, i, -1, None)
                send(turn, 6 + 4 * n, i, -1, 0, (0, 1))
                share(turn, i, -1)
                arrive(turn, 5 + 4 * n, i, 1, None)
                send(turn, 7 + 4 * n, i, 1, 1, (0, -1))
                share(turn, i, 1)

        def finish(n, i):
            for turn in range(2):
                arrive(turn, 6 + 4 * n, i, 2, 0)
                arrive(turn, 7 + 4 * n, i, 2, 1)
                share(turn, i, 2)

        for turn in range(2):
            send(turn, 0, 0, 0, None, (1, 0))
            send(turn, 1, 0, 0, None, (-1, 0))
        spread(0, 0)
        for turn in range(2):
            share(turn, 0, 0)
        yield
        for turn in range(2):
            arrive(turn, 0, -1, 0, None)
            send(turn, 2, -1, 0, 0, (1, 0))
            arrive(turn, 1, 1, 0, None)
            send(turn, 3, 1, 0, 1, (-1, 0))
        spread(1, -1)
        spread(2, 1)
        for turn in range(2):
            share(turn, -1, 0)
            share(turn, 1, 0)
        yield
        relay(0, 0)
        for turn in range(2):
            arrive(turn, 2, 2, 0, 0)
            arrive(turn, 3, 2, 0, 1)
        spread(3, 2)
        for turn in range(2):
            share(turn, 2, 0)
        yield
        relay(1, -1)
        relay(2, 1)
        yield
        relay(3, 2)
        finish(0, 0)
        yield
        finish(1, -1)
        finish(2, 1)
        finish(3, 2)

    def ring_steps():
        size = FEAT // 2

        def region(t, part):
            return rows.at[rem(z + t + Z, Z), pl.ds(part * size, size)]

        def send(t, way, part):
            ref = region(-t * way, part)
            sem = z_recv.at[(0 if way > 0 else 16) + 2 * t + part]
            copy_to(ref, ref, z_send, sem, device(x, y, up if way > 0 else down, core)).start()

        def arrive(t, way, part):
            ref = region(-t * way, part)
            sem = z_recv.at[(0 if way > 0 else 16) + 2 * (t - 1) + part]
            copy_to(ref, ref, z_send, sem, here).wait_recv()

        for part in range(2):
            send(0, 1, part)
            send(0, -1, part)
        yield
        for t in range(1, HALF):
            for part in range(2):
                for way in (1, -1):
                    arrive(t, way, part)
                    if t < HALF - 1 or part == (0 if way > 0 else 1):
                        send(t, way, part)
            yield
        arrive(HALF, 1, 0)
        arrive(HALF, -1, 1)

    for _ in plane_steps(0, FEAT, EIG):
        pass
    gone = copy_to(parts.at[pl.ds(0, REP - 1)], landed.at[pl.ds(0, REP - 1)], part_send, part_recv, here)
    gone.wait_recv()
    me = x * Y + y
    for p in range(REP):
        piece = landed[p, :PART, :] * ROOT
        rows[z, p * PART : (p + 1) * PART] = piece
        cols[me, core, p * PART : (p + 1) * PART] = piece
    ring, plane = ring_steps(), plane_steps(1, 0, FEAT)
    going = True
    while going:
        going = next(ring, "end") != "end"
        going = next(plane, "end") != "end" or going
    own_scale[...] = jnp.broadcast_to(scale_of(rows[z]), own_scale.shape)

    gone.wait_send()
    copy_to(lists, far_lists, list_send, list_recv, here).wait()
    fill = rows.at[pl.ds(0, Z - 1)]
    copy_to(fill, fill, z_send, z_recv.at[0], here).wait_send()
    fill = cols.at[pl.ds(0, PLANE - 1), core]
    copy_to(fill, fill, xy_send, xy_recv.at[0, 0], here).wait_send()
    fill = cols.at[:, core]
    copy_to(fill, fill, pair_send, pair_recv, here).wait_send()
    fill = cols.at[:, other]
    copy_to(fill, fill, pair_send, pair_recv, here).wait_recv()


def halves(value):
    high = value.astype(jnp.bfloat16)
    low = (value - high.astype(jnp.float32)).astype(jnp.bfloat16)
    return high, low


def compute_kernel(listed, rows, cols, out, row_ops, col_ops, vec_ops, picks):
    n_rows, n_cols = rows.shape[0], cols.shape[0]

    @pl.loop(0, n_rows)
    def _(r):
        high, low = halves(rows[r])
        both = jnp.concatenate([high.astype(jnp.float32), low.astype(jnp.float32)], axis=0)
        flipped = both.T.astype(jnp.bfloat16)
        row_ops[r, :, : 2 * FEAT] = flipped
        row_ops[r, :, 2 * FEAT :] = flipped

    @pl.loop(0, n_cols)
    def _(q):
        coords = cols[q, :FEAT]
        high, low = halves(coords)
        col_ops[q, :FEAT] = high
        col_ops[q, FEAT : 2 * FEAT] = high
        col_ops[q, 2 * FEAT : 3 * FEAT] = low
        col_ops[q, 3 * FEAT :] = low
        vecs = cols[q, FEAT:] * scale_of(coords)
        high, low = halves(vecs.T)
        vec_ops[q, 0] = high
        vec_ops[q, 1] = low

    vec_ops[n_cols] = jnp.zeros_like(vec_ops[n_cols])
    col_ops[n_cols] = jnp.zeros_like(col_ops[n_cols])

    @pl.loop(0, n_rows)
    def _(r):
        count = jnp.int32(0)
        for q in range(n_cols):
            picks[count] = q
            count = count + listed[r, q]
        picks[count] = n_cols
        out[r] = jnp.zeros_like(out[r])

        @pl.loop(0, (count + 1) // 2)
        def _(step):
            a, b = picks[2 * step], picks[2 * step + 1]
            col = jnp.concatenate([col_ops[a], col_ops[b]], axis=1)
            power = jnp.dot(row_ops[r], col, preferred_element_type=jnp.float32)
            high, low = halves(jnp.exp2(power))
            vec_high = jnp.concatenate([vec_ops[a, 0], vec_ops[b, 0]], axis=0)
            vec_low = jnp.concatenate([vec_ops[a, 1], vec_ops[b, 1]], axis=0)
            out[r] += (
                jnp.dot(high, vec_high, preferred_element_type=jnp.float32)
                + jnp.dot(high, vec_low, preferred_element_type=jnp.float32)
                + jnp.dot(low, vec_high, preferred_element_type=jnp.float32)
            )


def reduce_kernel(partial, own_scale, out, up_in, down_in, up_sum, down_sum, up_send, up_recv, down_send, down_recv):
    _, _, core, x, y, z = place()
    here = device(x, y, z, core)
    up, down = device(x, y, rem(z + 1, Z), core), device(x, y, rem(z + Z - 1, Z), core)
    barrier = pltpu.get_barrier_semaphore()
    for mate in (up, down):
        pl.semaphore_signal(barrier, inc=1, device_id=mate, device_id_type=MESH)
    pl.semaphore_wait(barrier, 2)
    size = BLOCK // 2
    ways = (
        (1, up, up_in, up_sum, up_send, up_recv),
        (-1, down, down_in, down_sum, down_send, down_recv),
    )

    def slot(step, part):
        return 2 * step - part

    for step in range(HALF):
        for lead in range(2):
            for way, to, landing, sums, send, recv in ways:
                if step == 0 and lead == 1:
                    continue
                part = lead if way > 0 else 1 - lead
                mine = partial.at[rem(z + way * (HALF - step) + Z, Z), pl.ds(part * size, size)]
                first = step == 0 if lead == 0 else step == 1
                at = slot(step, lead)
                if first:
                    src = mine
                else:
                    before = slot(step - 1, lead)
                    ref = landing.at[before]
                    copy_to(ref, ref, send, recv.at[before], here).wait_recv()
                    sums[at] = mine[...] + landing[before]
                    src = sums.at[at]
                copy_to(src, landing.at[at], send, recv.at[at], to).start()
    for part in range(2):
        total = partial[z, part * size : (part + 1) * size]
        for way, to, landing, sums, send, recv in ways:
            lead = part if way > 0 else 1 - part
            at = slot(HALF - 1, lead)
            ref = landing.at[at]
            copy_to(ref, ref, send, recv.at[at], here).wait_recv()
            total = total + landing[at]
        out[:, part * size : (part + 1) * size] = total.T * own_scale[:1, part * size : (part + 1) * size]
    for way, to, landing, sums, send, recv in ways:
        copy_to(landing, landing, send, recv.at[0], here).wait_send()


def shards(coords, eigvecs, nbr_list, nbr_count):
    f32 = jnp.float32
    vmem = pl.BlockSpec(memory_space=pltpu.VMEM)
    dma = pltpu.SemaphoreType.DMA
    _, rep, core, _, _, z = place()
    zh, zl = z // HALF, rem(z, HALF)

    parts = coords.reshape(PART, REP, BLOCK).transpose(1, 0, 2)
    parts = jnp.pad(parts, ((0, 0), (0, PART_PAD - PART), (0, 0)))
    slots = lax.broadcasted_iota(jnp.int32, nbr_list.shape, 1)
    lists = jnp.where(slots < nbr_count[:, None], nbr_list, -1)

    rows, cols, far_lists, own_scale = pl.pallas_call(
        gather_kernel,
        out_shape=(
            jax.ShapeDtypeStruct((Z, FEAT, BLOCK), f32),
            jax.ShapeDtypeStruct((PLANE, 2, PANEL, BLOCK), f32),
            jax.ShapeDtypeStruct(lists.shape, jnp.int32),
            jax.ShapeDtypeStruct((8, BLOCK), f32),
        ),
        in_specs=[vmem] * 3,
        out_specs=(vmem,) * 4,
        scratch_shapes=[
            pltpu.VMEM((REP, PART_PAD, BLOCK), f32),
            dma, dma, dma, dma, dma, dma((32,)), dma, dma((2, 40)), dma, dma,
        ],
        compiler_params=pltpu.CompilerParams(collective_id=0, has_side_effects=True),
    )(parts, eigvecs, lists)

    both = jnp.stack([lists, far_lists]).reshape(2, HALF, 2, BLOCK)
    both = jnp.where(core == 0, both[:, :, 0], both[:, :, 1])
    wanted = jnp.where(zh == 0, both, both[::-1]).reshape(Z, BLOCK)
    q = jnp.arange(2 * PLANE, dtype=jnp.int32)
    names = ((q // 2) * 2 + zh) * REP + zl * 2 + q % 2
    listed = jnp.any(wanted[:, None, :] == names[None, :, None], axis=-1).astype(jnp.int32)

    n_cols = 2 * PLANE
    partial = pl.pallas_call(
        compute_kernel,
        out_shape=jax.ShapeDtypeStruct((Z, BLOCK, EIG), f32),
        in_specs=[pl.BlockSpec(memory_space=pltpu.SMEM), vmem, vmem],
        out_specs=vmem,
        scratch_shapes=[
            pltpu.VMEM((Z, BLOCK, 4 * FEAT), jnp.bfloat16),
            pltpu.VMEM((n_cols + 1, 4 * FEAT, BLOCK), jnp.bfloat16),
            pltpu.VMEM((n_cols + 1, 2, BLOCK, EIG), jnp.bfloat16),
            pltpu.SMEM((n_cols + 8,), jnp.int32),
        ],
    )(listed, rows, cols.reshape(n_cols, PANEL, BLOCK))

    size = BLOCK // 2
    return pl.pallas_call(
        reduce_kernel,
        out_shape=jax.ShapeDtypeStruct((EIG, BLOCK), f32),
        in_specs=[vmem] * 2,
        out_specs=vmem,
        scratch_shapes=[pltpu.VMEM((2 * HALF - 1, size, EIG), f32)] * 4
        + [dma, dma((2 * HALF - 1,)), dma, dma((2 * HALF - 1,))],
        compiler_params=pltpu.CompilerParams(collective_id=1, has_side_effects=True),
    )(partial, own_scale)


def solution(mesh):
    return jax.shard_map(
        shards,
        mesh=mesh,
        in_specs=(P("rep", "blk"), P(None, ("blk", "rep")), P("blk", None), P("blk")),
        out_specs=P(None, ("blk", "rep")),
        check_vma=False,
    )
```

```python
import math

import jax
import jax.numpy as jnp
from jax import lax
from jax.experimental import pallas as pl
from jax.experimental.pallas import tpu as pltpu
from jax.sharding import PartitionSpec as P

MESH = pl.DeviceIdType.MESH
X, Y, Z = 4, 4, 16
HALF = Z // 2
PLANE = X * Y
FEAT, EIG, BLOCK = 192, 128, 128
PANEL = FEAT + EIG
PART = 12
PART_PAD = 16
REP = 16
COLS = 2 * PLANE
WIDE = COLS * BLOCK
CHUNK = 1024
PIECES = 4
ROOT = math.sqrt(2.0 * math.log2(math.e) / FEAT)
UNLISTED = -1024.0
OFFSETS = [0, HALF] + [o for s in range(1, HALF) for o in (HALF - s, s - HALF)]
SHIFTS = (0, -1, 1, 2)


def rem(a, b):
    return lax.rem(a, jnp.int32(b))


def place():
    blk, rep = lax.axis_index("blk"), lax.axis_index("rep")
    core, zl = rem(rep, 2), rep // 2
    zh, xy = rem(blk, 2), blk // 2
    return blk, rep, core, xy // Y, rem(xy, Y), zh * HALF + zl


def device(x, y, z, core):
    return {"blk": (x * Y + y) * 2 + z // HALF, "rep": rem(z, HALF) * 2 + core}


def copy_to(src, dst, send, recv, where):
    return pltpu.make_async_remote_copy(
        src_ref=src, dst_ref=dst, send_sem=send, recv_sem=recv, device_id=where, device_id_type=MESH
    )


def halves(value):
    high = value.astype(jnp.bfloat16)
    low = (value - high.astype(jnp.float32)).astype(jnp.bfloat16)
    return high, low


def dot(a, b):
    return jnp.dot(a, b, preferred_element_type=jnp.float32)


def half_norm(x):
    return 0.5 * jnp.sum(x * x, axis=0, keepdims=True)


def kernel(
    parts, vecs, lists, out,
    landed, far_lists, own_vecs, rows, cols, row_ops, col_ops, vec_ops, col_norms, row_lists, shifts,
    partial, up_in, down_in, up_sum, down_sum,
    part_send, part_recv, list_send, list_recv, z_send, z_recv, xy_send, xy_recv, pair_send, pair_recv,
    up_send, up_recv, down_send, down_recv,
):
    blk, rep, core, x, y, z = place()
    other = 1 - core
    here = device(x, y, z, core)
    up, down = device(x, y, rem(z + 1, Z), core), device(x, y, rem(z + Z - 1, Z), core)
    far = device(x, y, rem(z + HALF, Z), core)

    barrier = pltpu.get_barrier_semaphore()
    mates = [{"blk": blk, "rep": rem(rep + d, REP)} for d in range(1, REP)] + [up, down, far]
    mates += [device(rem(x + d, X), y, z, core) for d in (1, X - 1)]
    mates += [device(x, rem(y + d, Y), z, core) for d in (1, Y - 1)]
    for mate in mates:
        pl.semaphore_signal(barrier, inc=1, device_id=mate, device_id_type=MESH)
    own_vecs[...] = vecs[...].T
    cols[x * Y + y, core, FEAT:] = own_vecs[...]
    landed[rep] = parts[rep]
    up_in[0] = jnp.zeros_like(up_in[0])
    down_in[0] = jnp.zeros_like(down_in[0])
    pl.semaphore_wait(barrier, len(mates))

    for d in range(1, REP):
        to = rem(rep + d, REP)
        copy_to(parts.at[to], landed.at[rep], part_send, part_recv, {"blk": blk, "rep": to}).start()

    def spot(dx, dy):
        return rem(x + dx + X, X), rem(y + dy + Y, Y)

    def slot(dx, dy, k):
        return (SHIFTS.index(dx) * len(SHIFTS) + SHIFTS.index(dy)) * 2 + k

    def ready(phase, dx, dy, k):
        sx, sy = spot(dx, dy)
        q = slot(dx, dy, k)
        panel = cols.at[sx * Y + sy, core if k == 0 else other]
        if phase == 0:
            high, low = halves(panel[FEAT:])
            vec_ops[q * BLOCK : (q + 1) * BLOCK, :EIG] = high
            vec_ops[q * BLOCK : (q + 1) * BLOCK, EIG:] = low
            return
        coords = panel[:FEAT]
        high, low = halves(coords)
        lanes = slice(q * BLOCK, (q + 1) * BLOCK)
        col_ops[:FEAT, lanes] = high
        col_ops[FEAT : 2 * FEAT, lanes] = high
        col_ops[2 * FEAT : 3 * FEAT, lanes] = low
        col_ops[3 * FEAT :, lanes] = low
        col_norms[:, lanes] = jnp.broadcast_to(half_norm(coords), (8, BLOCK))

    def plane_steps(phase, base, size):
        half, quarter = size // 2, size // 4

        def region(turn, i, j, part, owner=core):
            sx, sy = spot(i, j) if turn == 0 else spot(j, i)
            start, count = base + turn * half, half
            if part is not None:
                start, count = start + part * quarter, quarter
            return cols.at[sx * Y + sy, owner, pl.ds(start, count)]

        def source(turn, i, j, ref):
            return own_vecs.at[pl.ds(turn * half, half)] if phase == 0 and (i, j) == (0, 0) else ref

        def send(turn, n, i, j, part, to):
            tx, ty = spot(*to) if turn == 0 else spot(to[1], to[0])
            ref = region(turn, i, j, part)
            sem = xy_recv.at[phase, turn * 20 + n]
            copy_to(source(turn, i, j, ref), ref, xy_send, sem, device(tx, ty, z, core)).start()

        def arrive(turn, n, i, j, part):
            ref = region(turn, i, j, part)
            copy_to(ref, ref, xy_send, xy_recv.at[phase, turn * 20 + n], here).wait_recv()

        def at(turn, i, j):
            dx, dy = (i, j) if turn == 0 else (j, i)
            return phase * COLS + turn * PLANE + slot(dx, dy, 0) // 2

        def share(turn, i, j):
            ref = region(turn, i, j, None)
            copy_to(source(turn, i, j, ref), ref, pair_send, pair_recv.at[at(turn, i, j)], device(x, y, z, other)).start()

        def take(i, j):
            for turn in range(2):
                a, b = (i, j) if turn == 0 else (j, i)
                ref = region(turn, a, b, None, other)
                copy_to(ref, ref, pair_send, pair_recv.at[at(turn, a, b)], here).wait_recv()
            ready(phase, i, j, 1)

        def spread(n, i):
            for turn in range(2):
                send(turn, 4 + 4 * n, i, 0, None, (0, 1))
                send(turn, 5 + 4 * n, i, 0, None, (0, -1))

        def relay(n, i):
            for turn in range(2):
                arrive(turn, 4 + 4 * n, i, -1, None)
                send(turn, 6 + 4 * n, i, -1, 0, (0, 1))
                share(turn, i, -1)
                arrive(turn, 5 + 4 * n, i, 1, None)
                send(turn, 7 + 4 * n, i, 1, 1, (0, -1))
                share(turn, i, 1)

        def finish(n, i):
            for turn in range(2):
                arrive(turn, 6 + 4 * n, i, 2, 0)
                arrive(turn, 7 + 4 * n, i, 2, 1)
                share(turn, i, 2)

        for turn in range(2):
            send(turn, 0, 0, 0, None, (1, 0))
            send(turn, 1, 0, 0, None, (-1, 0))
        spread(0, 0)
        for turn in range(2):
            share(turn, 0, 0)
        ready(phase, 0, 0, 0)
        yield
        for turn in range(2):
            arrive(turn, 0, -1, 0, None)
            send(turn, 2, -1, 0, 0, (1, 0))
            arrive(turn, 1, 1, 0, None)
            send(turn, 3, 1, 0, 1, (-1, 0))
        spread(1, -1)
        spread(2, 1)
        for turn in range(2):
            share(turn, -1, 0)
            share(turn, 1, 0)
        take(0, 0)
        yield
        relay(0, 0)
        for turn in range(2):
            arrive(turn, 2, 2, 0, 0)
            arrive(turn, 3, 2, 0, 1)
        spread(3, 2)
        for turn in range(2):
            share(turn, 2, 0)
        for a, b in ((0, 1), (0, -1), (1, 0), (-1, 0)):
            ready(phase, a, b, 0)
        yield
        relay(1, -1)
        relay(2, 1)
        for a in (-1, 1):
            for b in (-1, 1):
                ready(phase, a, b, 0)
        for a, b in ((0, 1), (0, -1), (1, 0), (-1, 0)):
            take(a, b)
        yield
        relay(3, 2)
        finish(0, 0)
        ready(phase, 0, 2, 0)
        ready(phase, 2, 0, 0)
        for a in (-1, 1):
            for b in (-1, 1):
                take(a, b)
        yield
        finish(1, -1)
        finish(2, 1)
        for a in (-1, 1):
            ready(phase, a, 2, 0)
            ready(phase, 2, a, 0)
        take(0, 2)
        take(2, 0)
        yield
        finish(3, 2)
        ready(phase, 2, 2, 0)
        for a in (-1, 1):
            take(a, 2)
            take(2, a)
        take(2, 2)

    def row_ready(offset):
        s = OFFSETS.index(offset)
        high, low = halves(rows[rem(z + offset + Z, Z)])
        both = jnp.concatenate([high.astype(jnp.float32), low.astype(jnp.float32)], axis=0)
        flipped = both.T.astype(jnp.bfloat16)
        place_at = slice(s % 2 * BLOCK, (s % 2 + 1) * BLOCK)
        row_ops[s // 2, place_at, : 2 * FEAT] = flipped
        row_ops[s // 2, place_at, 2 * FEAT :] = flipped

    def ring_steps():
        size = FEAT // PIECES

        def region(t, part):
            return rows.at[rem(z + t + Z, Z), pl.ds(part * size, size)]

        def send(t, way, part):
            ref = region(-t * way, part)
            sem = z_recv.at[(0 if way > 0 else HALF * PIECES) + t * PIECES + part]
            copy_to(ref, ref, z_send, sem, up if way > 0 else down).start()

        def arrive(t, way, part):
            ref = region(-t * way, part)
            sem = z_recv.at[(0 if way > 0 else HALF * PIECES) + (t - 1) * PIECES + part]
            copy_to(ref, ref, z_send, sem, here).wait_recv()

        def goes(t, way, part):
            return t < HALF - 1 or (part < PIECES // 2) == (way > 0)

        for part in range(PIECES):
            send(0, 1, part)
            send(0, -1, part)
        row_ready(0)
        yield
        for t in range(1, HALF):
            for part in range(PIECES):
                for way in (1, -1):
                    arrive(t, way, part)
                    if goes(t, way, part):
                        send(t, way, part)
            row_ready(t)
            row_ready(-t)
            yield
        for part in range(PIECES):
            arrive(HALF, 1 if part < PIECES // 2 else -1, part)
        row_ready(HALF)

    first = plane_steps(0, FEAT, EIG)
    next(first)
    copy_to(lists, far_lists, list_send, list_recv, far).start()
    next(first)
    next(first)
    gone = copy_to(parts.at[pl.ds(0, REP - 1)], landed.at[pl.ds(0, REP - 1)], part_send, part_recv, here)
    gone.wait_recv()
    me = x * Y + y
    for p in range(REP):
        piece = landed[p, :PART, :] * ROOT
        rows[z, p * PART : (p + 1) * PART] = piece
        cols[me, core, p * PART : (p + 1) * PART] = piece
    going = [ring_steps(), plane_steps(1, 0, FEAT), first]
    while going:
        going = [steps for steps in going if next(steps, "end") != "end"]

    copy_to(lists, far_lists, list_send, list_recv, here).wait()
    for s, offset in enumerate(OFFSETS):
        there = rem(z + offset + Z, Z)
        at = rem(there, HALF) * 2 + core
        row_lists[s : s + 1] = jnp.where(there // HALF == z // HALF, lists[at], far_lists[at])
    picked = row_lists[...]
    for dx in SHIFTS:
        for dy in SHIFTS:
            for k in range(2):
                sx, sy = spot(dx, dy)
                name = ((sx * Y + sy) * 2 + z // HALF) * REP + rem(z, HALF) * 2 + (core if k == 0 else other)
                found = jnp.max(jnp.where(picked == name, 1.0, 0.0), axis=1, keepdims=True)
                shift = jnp.where(found > 0.5, 0.0, UNLISTED)
                q = slot(dx, dy, k)
                lanes = slice(q * BLOCK, (q + 1) * BLOCK)
                shifts[:, lanes] = jnp.broadcast_to(shift, (2 * HALF, BLOCK)) - col_norms[:1, lanes]

    size = BLOCK // 2
    ways = (
        (1, up, up_in, up_sum, up_send, up_recv),
        (-1, down, down_in, down_sum, down_send, down_recv),
    )

    @pl.loop(0, HALF)
    def _(s):
        def chunk(n, total):
            c0 = pl.multiple_of(n * CHUNK, CHUNK)
            lanes = pl.ds(c0, CHUNK)
            power = dot(row_ops[s], col_ops[:, lanes])
            top = power[:BLOCK] + shifts[pl.ds(2 * s, 1), lanes]
            low = power[BLOCK:] + shifts[pl.ds(2 * s + 1, 1), lanes]
            high, low = halves(jnp.exp2(jnp.concatenate([top, low], axis=0)))
            ops = vec_ops[lanes]
            wide = dot(high, ops)
            return total + wide[:, :EIG] + wide[:, EIG:] + dot(low, ops[:, :EIG])

        zero = jnp.zeros((2 * BLOCK, EIG), jnp.float32)
        partial[s] = lax.fori_loop(0, WIDE // CHUNK, chunk, zero)

        @pl.when(s == 0)
        def _():
            copy_to(partial.at[0, pl.ds(BLOCK, size)], up_in.at[1], up_send, up_recv.at[1], up).start()
            copy_to(partial.at[0, pl.ds(BLOCK + size, size)], down_in.at[1], down_send, down_recv.at[1], down).start()

        @pl.when(s > 0)
        def _():
            for lead in range(2):
                for way, to, landing, sums, send, recv in ways:
                    start = (0 if way > 0 else BLOCK) + (lead if way > 0 else 1 - lead) * size
                    at = 2 * s + 1 - lead
                    ref = landing.at[at - 2]

                    def wait(ref=ref, send=send, sem=recv.at[at - 2]):
                        copy_to(ref, ref, send, sem, here).wait_recv()

                    if lead == 0:
                        wait()
                    else:
                        pl.when(s > 1)(wait)
                    sums[at] = partial[s, start : start + size] + landing[at - 2]
                    copy_to(sums.at[at], landing.at[at], send, recv.at[at], to).start()

    own_scale = jnp.exp2(-half_norm(rows[z]))
    for part in range(2):
        here_rows = slice(part * size, (part + 1) * size)
        total = partial[0, here_rows]
        for way, to, landing, sums, send, recv in ways:
            at = 2 * HALF - 1 - (part if way > 0 else 1 - part)
            ref = landing.at[at]
            copy_to(ref, ref, send, recv.at[at], here).wait_recv()
            total = total + landing[at]
        out[:, here_rows] = total.T * own_scale[:, here_rows]

    for way, to, landing, sums, send, recv in ways:
        fill = landing.at[pl.ds(1, 2 * HALF - 1)]
        copy_to(fill, fill, send, recv.at[0], here).wait_send()
    gone.wait_send()
    fill = rows.at[pl.ds(0, Z - 1)]
    copy_to(fill, fill, z_send, z_recv.at[0], here).wait_send()
    fill = cols.at[pl.ds(0, PLANE - 1), core]
    copy_to(fill, fill, xy_send, xy_recv.at[0, 0], here).wait_send()
    fill = cols.at[:, core]
    copy_to(fill, fill, pair_send, pair_recv.at[0], here).wait_send()


def shards(coords, eigvecs, nbr_list, nbr_count):
    f32, bf16 = jnp.float32, jnp.bfloat16
    vmem = pl.BlockSpec(memory_space=pltpu.VMEM)
    dma = pltpu.SemaphoreType.DMA

    parts = coords.reshape(PART, REP, BLOCK).transpose(1, 0, 2)
    parts = jnp.pad(parts, ((0, 0), (0, PART_PAD - PART), (0, 0)))
    slots = lax.broadcasted_iota(jnp.int32, nbr_list.shape, 1)
    lists = jnp.where(slots < nbr_count[:, None], nbr_list, -1).reshape(REP, 1, BLOCK)

    sums = pltpu.VMEM((2 * HALF, BLOCK // 2, EIG), f32)
    return pl.pallas_call(
        kernel,
        out_shape=jax.ShapeDtypeStruct((EIG, BLOCK), f32),
        in_specs=[vmem] * 3,
        out_specs=vmem,
        scratch_shapes=[
            pltpu.VMEM((REP, PART_PAD, BLOCK), f32),
            pltpu.VMEM((REP, 1, BLOCK), jnp.int32),
            pltpu.VMEM((BLOCK, EIG), f32),
            pltpu.VMEM((Z, FEAT, BLOCK), f32),
            pltpu.VMEM((PLANE, 2, PANEL, BLOCK), f32),
            pltpu.VMEM((HALF, 2 * BLOCK, 4 * FEAT), bf16),
            pltpu.VMEM((4 * FEAT, WIDE), bf16),
            pltpu.VMEM((WIDE, 2 * EIG), bf16),
            pltpu.VMEM((8, WIDE), f32),
            pltpu.VMEM((2 * HALF, BLOCK), jnp.int32),
            pltpu.VMEM((2 * HALF, WIDE), f32),
            pltpu.VMEM((HALF, 2 * BLOCK, EIG), f32),
            sums, sums, sums, sums,
            dma, dma, dma, dma,
            dma, dma((2 * HALF * PIECES,)),
            dma, dma((2, 40)),
            dma, dma((2 * COLS,)),
            dma, dma((2 * HALF,)),
            dma, dma((2 * HALF,)),
        ],
        compiler_params=pltpu.CompilerParams(collective_id=0, has_side_effects=True),
    )(parts, eigvecs, lists)


def solution(mesh):
    return jax.shard_map(
        shards,
        mesh=mesh,
        in_specs=(P("rep", "blk"), P(None, ("blk", "rep")), P("blk", None), P("blk")),
        out_specs=P(None, ("blk", "rep")),
        check_vma=False,
    )
```

```python
import math

import jax
import jax.numpy as jnp
from jax import lax
from jax.experimental import pallas as pl
from jax.experimental.pallas import tpu as pltpu
from jax.sharding import PartitionSpec as P

MESH = pl.DeviceIdType.MESH
X, Y, Z = 4, 4, 16
HALF = Z // 2
PLANE = X * Y
FEAT, EIG, BLOCK = 192, 128, 128
PANEL = FEAT + EIG
PART = 12
PART_PAD = 16
REP = 16
COLS = 2 * PLANE
WIDE = COLS * BLOCK
PACK = HALF * PART
PIECES = 4
WAIT = 3
ROOT = math.sqrt(2.0 * math.log2(math.e) / FEAT)
UNLISTED = -1024.0
PLACES = [
    (0, 0), (0, 1), (0, -1), (1, 0), (-1, 0), (1, 1), (1, -1), (-1, 1),
    (-1, -1), (0, 2), (2, 0), (1, 2), (-1, 2), (2, 1), (2, -1), (2, 2),
]


def rem(a, b):
    return lax.rem(a, jnp.int32(b))


def place():
    blk, rep = lax.axis_index("blk"), lax.axis_index("rep")
    core, zl = rem(rep, 2), rep // 2
    zh, xy = rem(blk, 2), blk // 2
    return blk, rep, core, xy // Y, rem(xy, Y), zh * HALF + zl


def device(x, y, z, core):
    return {"blk": (x * Y + y) * 2 + z // HALF, "rep": rem(z, HALF) * 2 + core}


def copy_to(src, dst, send, recv, where):
    return pltpu.make_async_remote_copy(
        src_ref=src, dst_ref=dst, send_sem=send, recv_sem=recv, device_id=where, device_id_type=MESH
    )


def halves(value):
    high = value.astype(jnp.bfloat16)
    low = (value - high.astype(jnp.float32)).astype(jnp.bfloat16)
    return high, low


def dot(a, b):
    return jnp.dot(a, b, preferred_element_type=jnp.float32)


def half_norm(x):
    return 0.5 * jnp.sum(x * x, axis=0, keepdims=True)


def kernel(
    coords, vecs, names, counts, out,
    parts, packs, landed, lists, far_lists, rows, cols, row_ops, col_ops, vec_ops, row_lists, shifts,
    partial, up_in, down_in, up_sum, down_sum,
    part_send, part_recv, list_send, list_recv, z_send, z_recv, xy_send, xy_recv, pair_send, pair_recv,
    up_send, up_recv, down_send, down_recv, swap_send, swap_recv,
):
    blk, rep, core, x, y, z = place()
    other = 1 - core
    here = device(x, y, z, core)
    up, down = device(x, y, rem(z + 1, Z), core), device(x, y, rem(z + Z - 1, Z), core)
    far = device(x, y, rem(z + HALF, Z), core)

    barrier = pltpu.get_barrier_semaphore()
    mates = [{"blk": blk, "rep": rem(rep + d, REP)} for d in range(1, REP)] + [up, down, far]
    mates += [device(rem(x + d, X), y, z, core) for d in (1, X - 1)]
    mates += [device(x, rem(y + d, Y), z, core) for d in (1, Y - 1)]
    for mate in mates:
        pl.semaphore_signal(barrier, inc=1, device_id=mate, device_id_type=MESH)
    for p in range(REP):
        piece = coords[:, p * BLOCK : (p + 1) * BLOCK] * ROOT
        parts[p, :PART] = piece
        packs[p % 2, p // 2 * PART : (p // 2 + 1) * PART] = piece
        parts[p, PART:] = jnp.zeros((PART_PAD - PART, BLOCK), jnp.float32)
        used = lax.broadcasted_iota(jnp.int32, (1, BLOCK), 1) < counts[p]
        lists[p] = jnp.where(used, names[p : p + 1], -1)
    cols[x * Y + y, core, FEAT:] = vecs[...].T
    landed[rep] = parts[rep]
    rows[z, core] = packs[core]
    up_in[0] = jnp.zeros_like(up_in[0])
    down_in[0] = jnp.zeros_like(down_in[0])
    pl.semaphore_wait(barrier, len(mates))

    for d in range(1, REP):
        to = rem(rep + d, REP)
        copy_to(parts.at[to], landed.at[rep], part_send, part_recv, {"blk": blk, "rep": to}).start()
    copy_to(lists, far_lists, list_send, list_recv, far).start()

    def swap(landing):
        return copy_to(packs.at[other], landing, swap_send, swap_recv, device(x, y, z, other))

    swap(rows.at[z, core]).start()

    def spot(dx, dy):
        return rem(x + dx + X, X), rem(y + dy + Y, Y)

    def slot(dx, dy, k):
        return PLACES.index((dx, dy)) * 2 + k

    def ready(dx, dy, k):
        sx, sy = spot(dx, dy)
        q = slot(dx, dy, k)
        panel = cols.at[sx * Y + sy, core if k == 0 else other]
        high, low = halves(panel[FEAT:])
        vec_ops[q * BLOCK : (q + 1) * BLOCK, :EIG] = high
        vec_ops[q * BLOCK : (q + 1) * BLOCK, EIG:] = low
        block = panel[:FEAT]
        high, low = halves(block)
        lanes = slice(q * BLOCK, (q + 1) * BLOCK)
        col_ops[:FEAT, lanes] = high
        col_ops[FEAT : 2 * FEAT, lanes] = high
        col_ops[2 * FEAT : 3 * FEAT, lanes] = low
        col_ops[3 * FEAT :, lanes] = low
        name = ((sx * Y + sy) * 2 + z // HALF) * REP + rem(z, HALF) * 2 + (core if k == 0 else other)
        found = jnp.max(jnp.where(row_lists[...] == name, 1.0, 0.0), axis=-1, keepdims=True)
        shift = jnp.where(found > 0.5, 0.0, UNLISTED)
        shifts[:, :, :, lanes] = jnp.broadcast_to(shift, (HALF, 2, 1, BLOCK)) - half_norm(block)

    def pair_of(there):
        offset = rem(there - z + Z, Z)
        return jnp.where(offset >= HALF, offset - HALF, rem(HALF - offset + HALF, HALF)), offset // HALF

    def note_lists():
        copy_to(lists, far_lists, list_send, list_recv, here).wait()
        for there in range(Z):
            pair, side = pair_of(jnp.int32(there))
            at = there % HALF * 2 + core
            row_lists[pair, side] = jnp.where(there // HALF == z // HALF, lists[at], far_lists[at])

    def products(s):
        power = dot(row_ops[s].reshape(2 * BLOCK, 4 * FEAT), col_ops[...])
        power = [power[side * BLOCK : (side + 1) * BLOCK] + shifts[s, side] for side in range(2)]
        high, low = halves(jnp.exp2(jnp.concatenate(power, axis=0)))
        wide = dot(high, vec_ops[...])
        return wide[:, :EIG] + wide[:, EIG:] + dot(low, vec_ops[:, :EIG])

    def plane_steps():
        half, quarter = PANEL // 2, PANEL // 4

        def region(turn, i, j, part, owner=core):
            sx, sy = spot(i, j) if turn == 0 else spot(j, i)
            start, count = turn * half, half
            if part is not None:
                start, count = start + part * quarter, quarter
            return cols.at[sx * Y + sy, owner, pl.ds(start, count)]

        def send(turn, n, i, j, part, to):
            tx, ty = spot(*to) if turn == 0 else spot(to[1], to[0])
            ref = region(turn, i, j, part)
            sem = xy_recv.at[turn * 20 + n]
            copy_to(ref, ref, xy_send, sem, device(tx, ty, z, core)).start()

        def arrive(turn, n, i, j, part):
            ref = region(turn, i, j, part)
            copy_to(ref, ref, xy_send, xy_recv.at[turn * 20 + n], here).wait_recv()

        def at(turn, i, j):
            dx, dy = (i, j) if turn == 0 else (j, i)
            return turn * PLANE + slot(dx, dy, 0) // 2

        def share(turn, i, j):
            ref = region(turn, i, j, None)
            copy_to(ref, ref, pair_send, pair_recv.at[at(turn, i, j)], device(x, y, z, other)).start()

        def take(i, j):
            for turn in range(2):
                a, b = (i, j) if turn == 0 else (j, i)
                ref = region(turn, a, b, None, other)
                copy_to(ref, ref, pair_send, pair_recv.at[at(turn, a, b)], here).wait_recv()
            ready(i, j, 1)

        def spread(n, i):
            for turn in range(2):
                send(turn, 4 + 4 * n, i, 0, None, (0, 1))
                send(turn, 5 + 4 * n, i, 0, None, (0, -1))

        def relay(n, i):
            for turn in range(2):
                arrive(turn, 4 + 4 * n, i, -1, None)
                send(turn, 6 + 4 * n, i, -1, 0, (0, 1))
                share(turn, i, -1)
                arrive(turn, 5 + 4 * n, i, 1, None)
                send(turn, 7 + 4 * n, i, 1, 1, (0, -1))
                share(turn, i, 1)

        def finish(n, i):
            for turn in range(2):
                arrive(turn, 6 + 4 * n, i, 2, 0)
                arrive(turn, 7 + 4 * n, i, 2, 1)
                share(turn, i, 2)

        for turn in range(2):
            send(turn, 0, 0, 0, None, (1, 0))
            send(turn, 1, 0, 0, None, (-1, 0))
        spread(0, 0)
        for turn in range(2):
            share(turn, 0, 0)
        note_lists()
        ready(0, 0, 0)
        yield
        for turn in range(2):
            arrive(turn, 0, -1, 0, None)
            send(turn, 2, -1, 0, 0, (1, 0))
            arrive(turn, 1, 1, 0, None)
            send(turn, 3, 1, 0, 1, (-1, 0))
        spread(1, -1)
        spread(2, 1)
        for turn in range(2):
            share(turn, -1, 0)
            share(turn, 1, 0)
        take(0, 0)
        yield
        relay(0, 0)
        for turn in range(2):
            arrive(turn, 2, 2, 0, 0)
            arrive(turn, 3, 2, 0, 1)
        spread(3, 2)
        for turn in range(2):
            share(turn, 2, 0)
        for a, b in ((0, 1), (0, -1), (1, 0), (-1, 0)):
            ready(a, b, 0)
        yield
        relay(1, -1)
        relay(2, 1)
        for a in (-1, 1):
            for b in (-1, 1):
                ready(a, b, 0)
        for a, b in ((0, 1), (0, -1), (1, 0), (-1, 0)):
            take(a, b)
        yield
        relay(3, 2)
        finish(0, 0)
        ready(0, 2, 0)
        ready(2, 0, 0)
        for a in (-1, 1):
            for b in (-1, 1):
                take(a, b)
        yield
        finish(1, -1)
        finish(2, 1)
        for a in (-1, 1):
            ready(a, 2, 0)
            ready(2, a, 0)
        take(0, 2)
        take(2, 0)
        yield
        finish(3, 2)
        ready(2, 2, 0)
        for a in (-1, 1):
            take(a, 2)
            take(2, a)
        take(2, 2)

    def rows_ready():
        for there in range(Z):
            start = there % HALF * PART
            pieces = [
                rows[there // HALF * HALF + n // 2, n % 2, start : start + PART] for n in range(REP)
            ]
            high, low = halves(jnp.concatenate(pieces, axis=0))
            both = jnp.concatenate([high.astype(jnp.float32), low.astype(jnp.float32)], axis=0)
            flipped = both.T.astype(jnp.bfloat16)
            pair, side = pair_of(jnp.int32(there))
            row_ops[pair, side, :, : 2 * FEAT] = flipped
            row_ops[pair, side, :, 2 * FEAT :] = flipped

    def ring_steps():
        size = PACK // 2

        def region(t, part):
            owner = core if part < PIECES // 2 else other
            return rows.at[rem(z + t + Z, Z), owner, pl.ds(part % 2 * size, size)]

        def send(t, way, part):
            ref = region(-t * way, part)
            sem = z_recv.at[(0 if way > 0 else HALF * PIECES) + t * PIECES + part]
            copy_to(ref, ref, z_send, sem, up if way > 0 else down).start()

        def arrive(t, way, part):
            ref = region(-t * way, part)
            sem = z_recv.at[(0 if way > 0 else HALF * PIECES) + (t - 1) * PIECES + part]
            copy_to(ref, ref, z_send, sem, here).wait_recv()

        def goes(t, way, part):
            return t < HALF - 1 or (part < PIECES // 2) == (way > 0)

        for part in range(PIECES):
            if part == PIECES // 2:
                swap(rows.at[z, other]).wait()
            send(0, 1, part)
            send(0, -1, part)
        yield
        for t in range(1, HALF):
            for part in range(PIECES):
                for way in (1, -1):
                    arrive(t, way, part)
                    if goes(t, way, part):
                        send(t, way, part)
            yield
        for part in range(PIECES):
            arrive(HALF, 1 if part < PIECES // 2 else -1, part)

    def own_block():
        gone.wait_recv()
        for p in range(REP):
            cols[x * Y + y, core, p * PART : (p + 1) * PART] = landed[p, :PART, :]

    gone = copy_to(parts.at[pl.ds(0, REP - 1)], landed.at[pl.ds(0, REP - 1)], part_send, part_recv, here)
    ring, plane = ring_steps(), plane_steps()
    for step in range(WAIT):
        next(ring)
    own_block()
    next(plane)
    going = [ring, plane]
    while going:
        going = [steps for steps in going if next(steps, "end") != "end"]
    rows_ready()

    size = BLOCK // 2
    ways = (
        (1, up, up_in, up_sum, up_send, up_recv),
        (-1, down, down_in, down_sum, down_send, down_recv),
    )

    @pl.loop(0, HALF)
    def _(s):
        partial[s] = products(s)

        @pl.when(s == 0)
        def _():
            copy_to(partial.at[0, pl.ds(BLOCK, size)], up_in.at[1], up_send, up_recv.at[1], up).start()
            copy_to(partial.at[0, pl.ds(BLOCK + size, size)], down_in.at[1], down_send, down_recv.at[1], down).start()

        @pl.when(s > 0)
        def _():
            for lead in range(2):
                for way, to, landing, sums, send, recv in ways:
                    start = (0 if way > 0 else BLOCK) + (lead if way > 0 else 1 - lead) * size
                    at = 2 * s + 1 - lead
                    ref = landing.at[at - 2]

                    def wait(ref=ref, send=send, sem=recv.at[at - 2]):
                        copy_to(ref, ref, send, sem, here).wait_recv()

                    if lead == 0:
                        wait()
                    else:
                        pl.when(s > 1)(wait)
                    sums[at] = partial[s, start : start + size] + landing[at - 2]
                    copy_to(sums.at[at], landing.at[at], send, recv.at[at], to).start()

    own_scale = jnp.exp2(-half_norm(cols[x * Y + y, core, :FEAT]))
    for part in range(2):
        here_rows = slice(part * size, (part + 1) * size)
        total = partial[0, here_rows]
        for way, to, landing, sums, send, recv in ways:
            at = 2 * HALF - 1 - (part if way > 0 else 1 - part)
            ref = landing.at[at]
            copy_to(ref, ref, send, recv.at[at], here).wait_recv()
            total = total + landing[at]
        out[:, here_rows] = total.T * own_scale[:, here_rows]

    for way, to, landing, sums, send, recv in ways:
        fill = landing.at[pl.ds(1, 2 * HALF - 1)]
        copy_to(fill, fill, send, recv.at[0], here).wait_send()
    gone.wait_send()
    fill = rows.at[pl.ds(0, Z - 1)]
    copy_to(fill, fill, z_send, z_recv.at[0], here).wait_send()
    fill = cols.at[pl.ds(0, PLANE - 1), core]
    copy_to(fill, fill, xy_send, xy_recv.at[0], here).wait_send()
    fill = cols.at[:, core]
    copy_to(fill, fill, pair_send, pair_recv.at[0], here).wait_send()


def shards(coords, eigvecs, nbr_list, nbr_count):
    f32, bf16 = jnp.float32, jnp.bfloat16
    vmem = pl.BlockSpec(memory_space=pltpu.VMEM)
    dma = pltpu.SemaphoreType.DMA

    sums = pltpu.VMEM((2 * HALF, BLOCK // 2, EIG), f32)
    return pl.pallas_call(
        kernel,
        out_shape=jax.ShapeDtypeStruct((EIG, BLOCK), f32),
        in_specs=[vmem] * 3 + [pl.BlockSpec(memory_space=pltpu.SMEM)],
        out_specs=vmem,
        scratch_shapes=[
            pltpu.VMEM((REP, PART_PAD, BLOCK), f32),
            pltpu.VMEM((2, PACK, BLOCK), f32),
            pltpu.VMEM((REP, PART_PAD, BLOCK), f32),
            pltpu.VMEM((REP, 1, BLOCK), jnp.int32),
            pltpu.VMEM((REP, 1, BLOCK), jnp.int32),
            pltpu.VMEM((Z, 2, PACK, BLOCK), f32),
            pltpu.VMEM((PLANE, 2, PANEL, BLOCK), f32),
            pltpu.VMEM((HALF, 2, BLOCK, 4 * FEAT), bf16),
            pltpu.VMEM((4 * FEAT, WIDE), bf16),
            pltpu.VMEM((WIDE, 2 * EIG), bf16),
            pltpu.VMEM((HALF, 2, 1, BLOCK), jnp.int32),
            pltpu.VMEM((HALF, 2, 1, WIDE), f32),
            pltpu.VMEM((HALF, 2 * BLOCK, EIG), f32),
            sums, sums, sums, sums,
            dma, dma, dma, dma,
            dma, dma((2 * HALF * PIECES,)),
            dma, dma((40,)),
            dma, dma((COLS,)),
            dma, dma((2 * HALF,)),
            dma, dma((2 * HALF,)),
            dma, dma,
        ],
        compiler_params=pltpu.CompilerParams(collective_id=0, has_side_effects=True),
    )(coords, eigvecs, nbr_list, nbr_count)


def solution(mesh):
    return jax.shard_map(
        shards,
        mesh=mesh,
        in_specs=(P("rep", "blk"), P(None, ("blk", "rep")), P("blk", None), P("blk")),
        out_specs=P(None, ("blk", "rep")),
        check_vma=False,
    )
```

```python
import math

import jax
import jax.numpy as jnp
from jax import lax
from jax.experimental import pallas as pl
from jax.experimental.pallas import tpu as pltpu
from jax.sharding import PartitionSpec as P

MESH = pl.DeviceIdType.MESH
X, Y, Z = 4, 4, 16
HALF = Z // 2
PLANE = X * Y
FEAT, EIG, BLOCK = 192, 128, 128
PANEL = FEAT + EIG
PART = 12
REP = 16
COLS = 2 * PLANE
WIDE = COLS * BLOCK
PACK = HALF * PART
PIECES = 4
WAIT = 3
ROOT = math.sqrt(2.0 * math.log2(math.e) / FEAT)
UNLISTED = -1024.0
PLACES = [
    (0, 0), (0, 1), (0, -1), (1, 0), (-1, 0), (1, 1), (1, -1), (-1, 1),
    (-1, -1), (0, 2), (2, 0), (1, 2), (-1, 2), (2, 1), (2, -1), (2, 2),
]


def rem(a, b):
    return lax.rem(a, jnp.int32(b))


def place():
    blk, rep = lax.axis_index("blk"), lax.axis_index("rep")
    core, zl = rem(rep, 2), rep // 2
    zh, xy = rem(blk, 2), blk // 2
    return blk, rep, core, xy // Y, rem(xy, Y), zh * HALF + zl


def device(x, y, z, core):
    return {"blk": (x * Y + y) * 2 + z // HALF, "rep": rem(z, HALF) * 2 + core}


def copy_to(src, dst, send, recv, where):
    return pltpu.make_async_remote_copy(
        src_ref=src, dst_ref=dst, send_sem=send, recv_sem=recv, device_id=where, device_id_type=MESH
    )


def halves(value):
    high = value.astype(jnp.bfloat16)
    low = (value - high.astype(jnp.float32)).astype(jnp.bfloat16)
    return high, low


def dot(a, b):
    return jnp.dot(a, b, preferred_element_type=jnp.float32)


def half_norm(x):
    return 0.5 * jnp.sum(x * x, axis=0, keepdims=True)


def kernel(
    coords_in, vecs_in, names_in, counts, out,
    coords, vecs, names, in_sem,
    parts, packs, landed, lists, far_lists, rows, cols, row_ops, col_ops, vec_ops, row_lists, shifts,
    partial, up_in, down_in, up_sum, down_sum,
    part_send, part_recv, list_send, list_recv, z_send, z_recv, xy_send, xy_recv, pair_send, pair_recv,
    up_send, up_recv, down_send, down_recv, swap_send, swap_recv,
):
    blk, rep, core, x, y, z = place()
    other = 1 - core
    here = device(x, y, z, core)
    up, down = device(x, y, rem(z + 1, Z), core), device(x, y, rem(z + Z - 1, Z), core)
    far = device(x, y, rem(z + HALF, Z), core)

    barrier = pltpu.get_barrier_semaphore()
    mates = [{"blk": blk, "rep": rem(rep + d, REP)} for d in range(1, REP)] + [up, down, far]
    mates += [device(rem(x + d, X), y, z, core) for d in (1, X - 1)]
    mates += [device(x, rem(y + d, Y), z, core) for d in (1, Y - 1)]
    for mate in mates:
        pl.semaphore_signal(barrier, inc=1, device_id=mate, device_id_type=MESH)
    loads = [
        pltpu.make_async_copy(src, dst, in_sem.at[n])
        for n, (src, dst) in enumerate(((coords_in, coords), (names_in, names), (vecs_in, vecs)))
    ]
    for load in loads:
        load.start()
    for load in loads:
        load.wait()
    for p in range(REP):
        piece = coords[:, p * BLOCK : (p + 1) * BLOCK] * ROOT
        parts[p, :PART] = piece
        packs[p % 2, p // 2 * PART : (p // 2 + 1) * PART] = piece
        used = lax.broadcasted_iota(jnp.int32, (1, BLOCK), 1) < counts[p]
        lists[p] = jnp.where(used, names[p : p + 1], -1)
    cols[x * Y + y, core, FEAT:] = vecs[...].T
    landed[rep] = parts[rep]
    rows[z, core] = packs[core]
    up_in[0] = jnp.zeros_like(up_in[0])
    down_in[0] = jnp.zeros_like(down_in[0])
    pl.semaphore_wait(barrier, len(mates))

    for d in sorted(range(1, REP), key=lambda d: abs(d - HALF)):
        to = rem(rep + d, REP)
        copy_to(parts.at[to], landed.at[rep], part_send, part_recv, {"blk": blk, "rep": to}).start()
    copy_to(lists, far_lists, list_send, list_recv, far).start()

    def swap(landing):
        return copy_to(packs.at[other], landing, swap_send, swap_recv, device(x, y, z, other))

    swap(rows.at[z, core]).start()

    def spot(dx, dy):
        return rem(x + dx + X, X), rem(y + dy + Y, Y)

    def slot(dx, dy, k):
        return PLACES.index((dx, dy)) * 2 + k

    def ready(dx, dy, k):
        sx, sy = spot(dx, dy)
        q = slot(dx, dy, k)
        panel = cols.at[sx * Y + sy, core if k == 0 else other]
        high, low = halves(panel[FEAT:])
        vec_ops[q * BLOCK : (q + 1) * BLOCK, :EIG] = high
        vec_ops[q * BLOCK : (q + 1) * BLOCK, EIG:] = low
        block = panel[:FEAT]
        high, low = halves(block)
        lanes = slice(q * BLOCK, (q + 1) * BLOCK)
        col_ops[:FEAT, lanes] = high
        col_ops[FEAT : 2 * FEAT, lanes] = high
        col_ops[2 * FEAT : 3 * FEAT, lanes] = low
        col_ops[3 * FEAT :, lanes] = low
        name = ((sx * Y + sy) * 2 + z // HALF) * REP + rem(z, HALF) * 2 + (core if k == 0 else other)
        found = jnp.max(jnp.where(row_lists[...] == name, 1.0, 0.0), axis=-1, keepdims=True)
        shift = jnp.where(found > 0.5, 0.0, UNLISTED)
        shifts[:, :, :, lanes] = jnp.broadcast_to(shift, (HALF, 2, 1, BLOCK)) - half_norm(block)

    def pair_of(there):
        offset = rem(there - z + Z, Z)
        return jnp.where(offset >= HALF, offset - HALF, rem(HALF - offset + HALF, HALF)), offset // HALF

    def note_lists():
        copy_to(lists, far_lists, list_send, list_recv, here).wait()
        for there in range(Z):
            pair, side = pair_of(jnp.int32(there))
            at = there % HALF * 2 + core
            row_lists[pair, side] = jnp.where(there // HALF == z // HALF, lists[at], far_lists[at])

    def products(s):
        power = dot(row_ops[s].reshape(2 * BLOCK, 4 * FEAT), col_ops[...])
        power = [power[side * BLOCK : (side + 1) * BLOCK] + shifts[s, side] for side in range(2)]
        high, low = halves(jnp.exp2(jnp.concatenate(power, axis=0)))
        wide = dot(high, vec_ops[...])
        return wide[:, :EIG] + wide[:, EIG:] + dot(low, vec_ops[:, :EIG])

    def plane_steps():
        half, quarter = PANEL // 2, PANEL // 4

        def region(turn, i, j, part, owner=core):
            sx, sy = spot(i, j) if turn == 0 else spot(j, i)
            start, count = turn * half, half
            if part is not None:
                start, count = start + part * quarter, quarter
            return cols.at[sx * Y + sy, owner, pl.ds(start, count)]

        def send(turn, n, i, j, part, to):
            tx, ty = spot(*to) if turn == 0 else spot(to[1], to[0])
            ref = region(turn, i, j, part)
            sem = xy_recv.at[turn * 20 + n]
            copy_to(ref, ref, xy_send, sem, device(tx, ty, z, core)).start()

        def arrive(turn, n, i, j, part):
            ref = region(turn, i, j, part)
            copy_to(ref, ref, xy_send, xy_recv.at[turn * 20 + n], here).wait_recv()

        def at(turn, i, j):
            dx, dy = (i, j) if turn == 0 else (j, i)
            return turn * PLANE + slot(dx, dy, 0) // 2

        def share(turn, i, j):
            ref = region(turn, i, j, None)
            copy_to(ref, ref, pair_send, pair_recv.at[at(turn, i, j)], device(x, y, z, other)).start()

        def take(i, j):
            for turn in range(2):
                a, b = (i, j) if turn == 0 else (j, i)
                ref = region(turn, a, b, None, other)
                copy_to(ref, ref, pair_send, pair_recv.at[at(turn, a, b)], here).wait_recv()
            ready(i, j, 1)

        def spread(n, i):
            for turn in range(2):
                send(turn, 4 + 4 * n, i, 0, None, (0, 1))
                send(turn, 5 + 4 * n, i, 0, None, (0, -1))

        def relay(n, i):
            for turn in range(2):
                arrive(turn, 4 + 4 * n, i, -1, None)
                send(turn, 6 + 4 * n, i, -1, 0, (0, 1))
                share(turn, i, -1)
                arrive(turn, 5 + 4 * n, i, 1, None)
                send(turn, 7 + 4 * n, i, 1, 1, (0, -1))
                share(turn, i, 1)

        def finish(n, i):
            for turn in range(2):
                arrive(turn, 6 + 4 * n, i, 2, 0)
                arrive(turn, 7 + 4 * n, i, 2, 1)
                share(turn, i, 2)

        for turn in range(2):
            send(turn, 0, 0, 0, None, (1, 0))
            send(turn, 1, 0, 0, None, (-1, 0))
        spread(0, 0)
        for turn in range(2):
            share(turn, 0, 0)
        note_lists()
        ready(0, 0, 0)
        yield
        for turn in range(2):
            arrive(turn, 0, -1, 0, None)
            send(turn, 2, -1, 0, 0, (1, 0))
            arrive(turn, 1, 1, 0, None)
            send(turn, 3, 1, 0, 1, (-1, 0))
        spread(1, -1)
        spread(2, 1)
        for turn in range(2):
            share(turn, -1, 0)
            share(turn, 1, 0)
        take(0, 0)
        yield
        relay(0, 0)
        for turn in range(2):
            arrive(turn, 2, 2, 0, 0)
            arrive(turn, 3, 2, 0, 1)
        spread(3, 2)
        for turn in range(2):
            share(turn, 2, 0)
        for a, b in ((0, 1), (0, -1), (1, 0), (-1, 0)):
            ready(a, b, 0)
        yield
        relay(1, -1)
        relay(2, 1)
        for a in (-1, 1):
            for b in (-1, 1):
                ready(a, b, 0)
        for a, b in ((0, 1), (0, -1), (1, 0), (-1, 0)):
            take(a, b)
        yield
        relay(3, 2)
        finish(0, 0)
        ready(0, 2, 0)
        ready(2, 0, 0)
        for a in (-1, 1):
            for b in (-1, 1):
                take(a, b)
        yield
        finish(1, -1)
        finish(2, 1)
        for a in (-1, 1):
            ready(a, 2, 0)
            ready(2, a, 0)
        take(0, 2)
        take(2, 0)
        yield
        finish(3, 2)
        ready(2, 2, 0)
        for a in (-1, 1):
            take(a, 2)
            take(2, a)
        take(2, 2)

    def rows_ready():
        for there in range(Z):
            start = there % HALF * PART
            pieces = [
                rows[there // HALF * HALF + n // 2, n % 2, start : start + PART] for n in range(REP)
            ]
            high, low = halves(jnp.concatenate(pieces, axis=0))
            both = jnp.concatenate([high.astype(jnp.float32), low.astype(jnp.float32)], axis=0)
            flipped = both.T.astype(jnp.bfloat16)
            pair, side = pair_of(jnp.int32(there))
            row_ops[pair, side, :, : 2 * FEAT] = flipped
            row_ops[pair, side, :, 2 * FEAT :] = flipped

    def ring_steps():
        count = PIECES // 2
        size = PACK // count

        def region(t, part):
            owner = core if part < PIECES // 2 else other
            return rows.at[rem(z + t + Z, Z), owner, pl.ds(part % count * size, size)]

        def send(t, way, part):
            ref = region(-t * way, part)
            sem = z_recv.at[(0 if way > 0 else HALF * PIECES) + t * PIECES + part]
            copy_to(ref, ref, z_send, sem, up if way > 0 else down).start()

        def arrive(t, way, part):
            ref = region(-t * way, part)
            sem = z_recv.at[(0 if way > 0 else HALF * PIECES) + (t - 1) * PIECES + part]
            copy_to(ref, ref, z_send, sem, here).wait_recv()

        def goes(t, way, part):
            return t < HALF - 1 or (part < PIECES // 2) == (way > 0)

        for part in range(PIECES):
            if part == PIECES // 2:
                swap(rows.at[z, other]).wait()
            send(0, 1, part)
            send(0, -1, part)
        yield
        for t in range(1, HALF):
            for part in range(PIECES):
                for way in (1, -1):
                    arrive(t, way, part)
                    if goes(t, way, part):
                        send(t, way, part)
            yield
        for part in range(PIECES):
            arrive(HALF, 1 if part < PIECES // 2 else -1, part)

    def own_block():
        gone.wait_recv()
        for p in range(REP):
            cols[x * Y + y, core, p * PART : (p + 1) * PART] = landed[p, :PART, :]

    gone = copy_to(parts.at[pl.ds(0, REP - 1)], landed.at[pl.ds(0, REP - 1)], part_send, part_recv, here)
    ring, plane = ring_steps(), plane_steps()
    for step in range(WAIT):
        next(ring)
    own_block()
    next(plane)
    going = [ring, plane]
    while going:
        going = [steps for steps in going if next(steps, "end") != "end"]
    rows_ready()

    size = BLOCK // 2
    ways = (
        (1, up, up_in, up_sum, up_send, up_recv),
        (-1, down, down_in, down_sum, down_send, down_recv),
    )

    @pl.loop(0, HALF)
    def _(s):
        partial[s] = products(s)

        @pl.when(s == 0)
        def _():
            copy_to(partial.at[0, pl.ds(BLOCK, size)], up_in.at[1], up_send, up_recv.at[1], up).start()
            copy_to(partial.at[0, pl.ds(BLOCK + size, size)], down_in.at[1], down_send, down_recv.at[1], down).start()

        @pl.when(s > 0)
        def _():
            for lead in range(2):
                for way, to, landing, sums, send, recv in ways:
                    start = (0 if way > 0 else BLOCK) + (lead if way > 0 else 1 - lead) * size
                    at = 2 * s + 1 - lead
                    ref = landing.at[at - 2]

                    def wait(ref=ref, send=send, sem=recv.at[at - 2]):
                        copy_to(ref, ref, send, sem, here).wait_recv()

                    if lead == 0:
                        wait()
                    else:
                        pl.when(s > 1)(wait)
                    sums[at] = partial[s, start : start + size] + landing[at - 2]
                    copy_to(sums.at[at], landing.at[at], send, recv.at[at], to).start()

    own_scale = jnp.exp2(-half_norm(cols[x * Y + y, core, :FEAT]))
    for part in range(2):
        here_rows = slice(part * size, (part + 1) * size)
        total = partial[0, here_rows]
        for way, to, landing, sums, send, recv in ways:
            at = 2 * HALF - 1 - (part if way > 0 else 1 - part)
            ref = landing.at[at]
            copy_to(ref, ref, send, recv.at[at], here).wait_recv()
            total = total + landing[at]
        out[:, here_rows] = total.T * own_scale[:, here_rows]

    for way, to, landing, sums, send, recv in ways:
        fill = landing.at[pl.ds(1, 2 * HALF - 1)]
        copy_to(fill, fill, send, recv.at[0], here).wait_send()
    gone.wait_send()
    fill = rows.at[pl.ds(0, Z - 1)]
    copy_to(fill, fill, z_send, z_recv.at[0], here).wait_send()
    fill = cols.at[pl.ds(0, PLANE - 1), core]
    copy_to(fill, fill, xy_send, xy_recv.at[0], here).wait_send()
    fill = cols.at[:, core]
    copy_to(fill, fill, pair_send, pair_recv.at[0], here).wait_send()


def shards(coords, eigvecs, nbr_list, nbr_count):
    f32, bf16 = jnp.float32, jnp.bfloat16
    vmem = pl.BlockSpec(memory_space=pltpu.VMEM)
    dma = pltpu.SemaphoreType.DMA

    sums = pltpu.VMEM((2 * HALF, BLOCK // 2, EIG), f32)
    return pl.pallas_call(
        kernel,
        out_shape=jax.ShapeDtypeStruct((EIG, BLOCK), f32),
        in_specs=[pl.BlockSpec(memory_space=pl.ANY)] * 3 + [pl.BlockSpec(memory_space=pltpu.SMEM)],
        out_specs=vmem,
        scratch_shapes=[
            pltpu.VMEM((PART, REP * BLOCK), f32),
            pltpu.VMEM((EIG, BLOCK), f32),
            pltpu.VMEM((REP, BLOCK), jnp.int32),
            dma((3,)),
            pltpu.VMEM((REP, PART, BLOCK), f32),
            pltpu.VMEM((2, PACK, BLOCK), f32),
            pltpu.VMEM((REP, PART, BLOCK), f32),
            pltpu.VMEM((REP, 1, BLOCK), jnp.int32),
            pltpu.VMEM((REP, 1, BLOCK), jnp.int32),
            pltpu.VMEM((Z, 2, PACK, BLOCK), f32),
            pltpu.VMEM((PLANE, 2, PANEL, BLOCK), f32),
            pltpu.VMEM((HALF, 2, BLOCK, 4 * FEAT), bf16),
            pltpu.VMEM((4 * FEAT, WIDE), bf16),
            pltpu.VMEM((WIDE, 2 * EIG), bf16),
            pltpu.VMEM((HALF, 2, 1, BLOCK), jnp.int32),
            pltpu.VMEM((HALF, 2, 1, WIDE), f32),
            pltpu.VMEM((HALF, 2 * BLOCK, EIG), f32),
            sums, sums, sums, sums,
            dma, dma, dma, dma,
            dma, dma((2 * HALF * PIECES,)),
            dma, dma((40,)),
            dma, dma((COLS,)),
            dma, dma((2 * HALF,)),
            dma, dma((2 * HALF,)),
            dma, dma,
        ],
        compiler_params=pltpu.CompilerParams(collective_id=0, has_side_effects=True),
    )(coords, eigvecs, nbr_list, nbr_count)


def solution(mesh):
    return jax.shard_map(
        shards,
        mesh=mesh,
        in_specs=(P("rep", "blk"), P(None, ("blk", "rep")), P("blk", None), P("blk")),
        out_specs=P(None, ("blk", "rep")),
        check_vma=False,
    )
```

```python
import math

import jax
import jax.numpy as jnp
from jax import lax
from jax.experimental import pallas as pl
from jax.experimental.pallas import tpu as pltpu
from jax.sharding import PartitionSpec as P

MESH = pl.DeviceIdType.MESH
X, Y, Z = 4, 4, 16
HALF = Z // 2
PLANE = X * Y
FEAT, EIG, BLOCK = 192, 128, 128
PANEL = FEAT + EIG
PART = 12
REP = 16
COLS = 2 * PLANE
WIDE = COLS * BLOCK
PACK = HALF * PART
PIECES = 4
WAIT = 2
ROOT = math.sqrt(2.0 * math.log2(math.e) / FEAT)
UNLISTED = -1024.0
PLACES = [
    (0, 0), (0, 1), (0, -1), (1, 0), (-1, 0), (1, 1), (1, -1), (-1, 1),
    (-1, -1), (0, 2), (2, 0), (1, 2), (-1, 2), (2, 1), (2, -1), (2, 2),
]


def rem(a, b):
    return lax.rem(a, jnp.int32(b))


def place():
    blk, rep = lax.axis_index("blk"), lax.axis_index("rep")
    core, zl = rem(rep, 2), rep // 2
    zh, xy = rem(blk, 2), blk // 2
    return blk, rep, core, xy // Y, rem(xy, Y), zh * HALF + zl


def device(x, y, z, core):
    return {"blk": (x * Y + y) * 2 + z // HALF, "rep": rem(z, HALF) * 2 + core}


def copy_to(src, dst, send, recv, where):
    return pltpu.make_async_remote_copy(
        src_ref=src, dst_ref=dst, send_sem=send, recv_sem=recv, device_id=where, device_id_type=MESH
    )


def halves(value):
    high = value.astype(jnp.bfloat16)
    low = (value - high.astype(jnp.float32)).astype(jnp.bfloat16)
    return high, low


def dot(a, b):
    return jnp.dot(a, b, preferred_element_type=jnp.float32)


def half_norm(x):
    return 0.5 * jnp.sum(x * x, axis=0, keepdims=True)


def kernel(
    coords_in, vecs_in, names_in, counts, out,
    coords, vecs, names, in_sem,
    parts, packs, landed, lists, far_lists, rows, cols, row_ops, col_ops, vec_ops, row_lists, shifts,
    partial, up_in, down_in, up_sum, down_sum,
    part_send, part_recv, list_send, list_recv, z_send, z_recv, xy_send, xy_recv, pair_send, pair_recv,
    up_send, up_recv, down_send, down_recv, swap_send, swap_recv,
):
    blk, rep, core, x, y, z = place()
    other = 1 - core
    here = device(x, y, z, core)
    up, down = device(x, y, rem(z + 1, Z), core), device(x, y, rem(z + Z - 1, Z), core)
    far = device(x, y, rem(z + HALF, Z), core)

    barrier = pltpu.get_barrier_semaphore()
    mates = [{"blk": blk, "rep": rem(rep + d, REP)} for d in range(1, REP)] + [up, down, far]
    mates += [device(rem(x + d, X), y, z, core) for d in (1, X - 1)]
    mates += [device(x, rem(y + d, Y), z, core) for d in (1, Y - 1)]
    for mate in mates:
        pl.semaphore_signal(barrier, inc=1, device_id=mate, device_id_type=MESH)
    loads = [
        pltpu.make_async_copy(src, dst, in_sem.at[n])
        for n, (src, dst) in enumerate(((coords_in, coords), (names_in, names), (vecs_in, vecs)))
    ]
    for load in loads:
        load.start()
    for load in loads:
        load.wait()
    for p in range(REP):
        piece = coords[:, p * BLOCK : (p + 1) * BLOCK] * ROOT
        parts[p, :PART] = piece
        packs[p % 2, p // 2 * PART : (p // 2 + 1) * PART] = piece
        used = lax.broadcasted_iota(jnp.int32, (1, BLOCK), 1) < counts[p]
        lists[p] = jnp.where(used, names[p : p + 1], -1)
    cols[x * Y + y, core, FEAT:] = vecs[...].T
    landed[rep] = parts[rep]
    rows[z, core] = packs[core]
    up_in[0] = jnp.zeros_like(up_in[0])
    down_in[0] = jnp.zeros_like(down_in[0])
    pl.semaphore_wait(barrier, len(mates))

    for d in sorted(range(1, REP), key=lambda d: abs(d - HALF)):
        to = rem(rep + d, REP)
        copy_to(parts.at[to], landed.at[rep], part_send, part_recv, {"blk": blk, "rep": to}).start()
    copy_to(lists, far_lists, list_send, list_recv, far).start()

    def swap(landing):
        return copy_to(packs.at[other], landing, swap_send, swap_recv, device(x, y, z, other))

    swap(rows.at[z, core]).start()

    def spot(dx, dy):
        return rem(x + dx + X, X), rem(y + dy + Y, Y)

    def slot(dx, dy, k):
        return PLACES.index((dx, dy)) * 2 + k

    def ready(dx, dy, k):
        sx, sy = spot(dx, dy)
        q = slot(dx, dy, k)
        panel = cols.at[sx * Y + sy, core if k == 0 else other]
        high, low = halves(panel[FEAT:])
        vec_ops[q * BLOCK : (q + 1) * BLOCK, :EIG] = high
        vec_ops[q * BLOCK : (q + 1) * BLOCK, EIG:] = low
        block = panel[:FEAT]
        high, low = halves(block)
        lanes = slice(q * BLOCK, (q + 1) * BLOCK)
        col_ops[:FEAT, lanes] = high
        col_ops[FEAT : 2 * FEAT, lanes] = high
        col_ops[2 * FEAT : 3 * FEAT, lanes] = low
        col_ops[3 * FEAT :, lanes] = low
        name = ((sx * Y + sy) * 2 + z // HALF) * REP + rem(z, HALF) * 2 + (core if k == 0 else other)
        found = jnp.max(jnp.where(row_lists[...] == name, 1.0, 0.0), axis=-1, keepdims=True)
        shift = jnp.where(found > 0.5, 0.0, UNLISTED)
        shifts[:, :, :, lanes] = jnp.broadcast_to(shift, (HALF, 2, 1, BLOCK)) - half_norm(block)

    def pair_of(there):
        offset = rem(there - z + Z, Z)
        return jnp.where(offset >= HALF, offset - HALF, rem(HALF - offset + HALF, HALF)), offset // HALF

    def note_lists():
        copy_to(lists, far_lists, list_send, list_recv, here).wait()
        for there in range(Z):
            pair, side = pair_of(jnp.int32(there))
            at = there % HALF * 2 + core
            row_lists[pair, side] = jnp.where(there // HALF == z // HALF, lists[at], far_lists[at])

    def products(s):
        power = dot(row_ops[s].reshape(2 * BLOCK, 4 * FEAT), col_ops[...])
        power = [power[side * BLOCK : (side + 1) * BLOCK] + shifts[s, side] for side in range(2)]
        high, low = halves(jnp.exp2(jnp.concatenate(power, axis=0)))
        wide = dot(high, vec_ops[...])
        return wide[:, :EIG] + wide[:, EIG:] + dot(low, vec_ops[:, :EIG])

    def plane_steps():
        half, quarter = PANEL // 2, PANEL // 4

        def region(turn, i, j, part, owner=core):
            sx, sy = spot(i, j) if turn == 0 else spot(j, i)
            start, count = turn * half, half
            if part is not None:
                start, count = start + part * quarter, quarter
            return cols.at[sx * Y + sy, owner, pl.ds(start, count)]

        def send(turn, n, i, j, part, to):
            tx, ty = spot(*to) if turn == 0 else spot(to[1], to[0])
            ref = region(turn, i, j, part)
            sem = xy_recv.at[turn * 20 + n]
            copy_to(ref, ref, xy_send, sem, device(tx, ty, z, core)).start()

        def arrive(turn, n, i, j, part):
            ref = region(turn, i, j, part)
            copy_to(ref, ref, xy_send, xy_recv.at[turn * 20 + n], here).wait_recv()

        def at(turn, i, j):
            dx, dy = (i, j) if turn == 0 else (j, i)
            return turn * PLANE + slot(dx, dy, 0) // 2

        def share(turn, i, j):
            ref = region(turn, i, j, None)
            copy_to(ref, ref, pair_send, pair_recv.at[at(turn, i, j)], device(x, y, z, other)).start()

        def take(i, j):
            for turn in range(2):
                a, b = (i, j) if turn == 0 else (j, i)
                ref = region(turn, a, b, None, other)
                copy_to(ref, ref, pair_send, pair_recv.at[at(turn, a, b)], here).wait_recv()
            ready(i, j, 1)

        def spread(n, i):
            for turn in range(2):
                send(turn, 4 + 4 * n, i, 0, None, (0, 1))
                send(turn, 5 + 4 * n, i, 0, None, (0, -1))

        def relay(n, i):
            for turn in range(2):
                arrive(turn, 4 + 4 * n, i, -1, None)
                send(turn, 6 + 4 * n, i, -1, 0, (0, 1))
                share(turn, i, -1)
                arrive(turn, 5 + 4 * n, i, 1, None)
                send(turn, 7 + 4 * n, i, 1, 1, (0, -1))
                share(turn, i, 1)

        def finish(n, i):
            for turn in range(2):
                arrive(turn, 6 + 4 * n, i, 2, 0)
                arrive(turn, 7 + 4 * n, i, 2, 1)
                share(turn, i, 2)

        for turn in range(2):
            send(turn, 0, 0, 0, None, (1, 0))
            send(turn, 1, 0, 0, None, (-1, 0))
        spread(0, 0)
        for turn in range(2):
            share(turn, 0, 0)
        note_lists()
        ready(0, 0, 0)
        yield
        for turn in range(2):
            arrive(turn, 0, -1, 0, None)
            send(turn, 2, -1, 0, 0, (1, 0))
            arrive(turn, 1, 1, 0, None)
            send(turn, 3, 1, 0, 1, (-1, 0))
        spread(1, -1)
        spread(2, 1)
        for turn in range(2):
            share(turn, -1, 0)
            share(turn, 1, 0)
        take(0, 0)
        yield
        relay(0, 0)
        for turn in range(2):
            arrive(turn, 2, 2, 0, 0)
            arrive(turn, 3, 2, 0, 1)
        spread(3, 2)
        for turn in range(2):
            share(turn, 2, 0)
        for a, b in ((0, 1), (0, -1), (1, 0), (-1, 0)):
            ready(a, b, 0)
        yield
        relay(1, -1)
        relay(2, 1)
        for a in (-1, 1):
            for b in (-1, 1):
                ready(a, b, 0)
        for a, b in ((0, 1), (0, -1), (1, 0), (-1, 0)):
            take(a, b)
        yield
        relay(3, 2)
        finish(0, 0)
        ready(0, 2, 0)
        ready(2, 0, 0)
        for a in (-1, 1):
            for b in (-1, 1):
                take(a, b)
        yield
        finish(1, -1)
        finish(2, 1)
        for a in (-1, 1):
            ready(a, 2, 0)
            ready(2, a, 0)
        take(0, 2)
        take(2, 0)
        yield
        finish(3, 2)
        ready(2, 2, 0)
        for a in (-1, 1):
            take(a, 2)
            take(2, a)
        take(2, 2)

    def rows_ready():
        for there in range(Z):
            start = there % HALF * PART
            pieces = [
                rows[there // HALF * HALF + n // 2, n % 2, start : start + PART] for n in range(REP)
            ]
            high, low = halves(jnp.concatenate(pieces, axis=0))
            both = jnp.concatenate([high.astype(jnp.float32), low.astype(jnp.float32)], axis=0)
            flipped = both.T.astype(jnp.bfloat16)
            pair, side = pair_of(jnp.int32(there))
            row_ops[pair, side, :, : 2 * FEAT] = flipped
            row_ops[pair, side, :, 2 * FEAT :] = flipped

    def ring_steps():
        count = PIECES // 2
        size = PACK // count

        def region(t, part):
            owner = core if part < PIECES // 2 else other
            return rows.at[rem(z + t + Z, Z), owner, pl.ds(part % count * size, size)]

        def send(t, way, part):
            ref = region(-t * way, part)
            sem = z_recv.at[(0 if way > 0 else HALF * PIECES) + t * PIECES + part]
            copy_to(ref, ref, z_send, sem, up if way > 0 else down).start()

        def arrive(t, way, part):
            ref = region(-t * way, part)
            sem = z_recv.at[(0 if way > 0 else HALF * PIECES) + (t - 1) * PIECES + part]
            copy_to(ref, ref, z_send, sem, here).wait_recv()

        def goes(t, way, part):
            return t < HALF - 1 or (part < PIECES // 2) == (way > 0)

        for part in range(PIECES):
            if part == PIECES // 2:
                swap(rows.at[z, other]).wait()
            send(0, 1, part)
            send(0, -1, part)
        yield
        for t in range(1, HALF):
            for part in range(PIECES):
                for way in (1, -1):
                    arrive(t, way, part)
                    if goes(t, way, part):
                        send(t, way, part)
            yield
        for part in range(PIECES):
            arrive(HALF, 1 if part < PIECES // 2 else -1, part)

    def own_block():
        gone.wait_recv()
        for p in range(REP):
            cols[x * Y + y, core, p * PART : (p + 1) * PART] = landed[p, :PART, :]

    gone = copy_to(parts.at[pl.ds(0, REP - 1)], landed.at[pl.ds(0, REP - 1)], part_send, part_recv, here)
    ring, plane = ring_steps(), plane_steps()
    for step in range(WAIT):
        next(ring)
    own_block()
    next(plane)
    going = [ring, plane]
    while going:
        going = [steps for steps in going if next(steps, "end") != "end"]
    rows_ready()

    size = BLOCK // 2
    ways = (
        (1, up, up_in, up_sum, up_send, up_recv),
        (-1, down, down_in, down_sum, down_send, down_recv),
    )

    @pl.loop(0, HALF)
    def _(s):
        partial[s] = products(s)

        @pl.when(s == 0)
        def _():
            copy_to(partial.at[0, pl.ds(BLOCK, size)], up_in.at[1], up_send, up_recv.at[1], up).start()
            copy_to(partial.at[0, pl.ds(BLOCK + size, size)], down_in.at[1], down_send, down_recv.at[1], down).start()

        @pl.when(s > 0)
        def _():
            for lead in range(2):
                for way, to, landing, sums, send, recv in ways:
                    start = (0 if way > 0 else BLOCK) + (lead if way > 0 else 1 - lead) * size
                    at = 2 * s + 1 - lead
                    ref = landing.at[at - 2]

                    def wait(ref=ref, send=send, sem=recv.at[at - 2]):
                        copy_to(ref, ref, send, sem, here).wait_recv()

                    if lead == 0:
                        wait()
                    else:
                        pl.when(s > 1)(wait)
                    sums[at] = partial[s, start : start + size] + landing[at - 2]
                    copy_to(sums.at[at], landing.at[at], send, recv.at[at], to).start()

    own_scale = jnp.exp2(-half_norm(cols[x * Y + y, core, :FEAT]))
    for part in range(2):
        here_rows = slice(part * size, (part + 1) * size)
        total = partial[0, here_rows]
        for way, to, landing, sums, send, recv in ways:
            at = 2 * HALF - 1 - (part if way > 0 else 1 - part)
            ref = landing.at[at]
            copy_to(ref, ref, send, recv.at[at], here).wait_recv()
            total = total + landing[at]
        out[:, here_rows] = total.T * own_scale[:, here_rows]

    for way, to, landing, sums, send, recv in ways:
        fill = landing.at[pl.ds(1, 2 * HALF - 1)]
        copy_to(fill, fill, send, recv.at[0], here).wait_send()
    gone.wait_send()
    fill = rows.at[pl.ds(0, Z - 1)]
    copy_to(fill, fill, z_send, z_recv.at[0], here).wait_send()
    fill = cols.at[pl.ds(0, PLANE - 1), core]
    copy_to(fill, fill, xy_send, xy_recv.at[0], here).wait_send()
    fill = cols.at[:, core]
    copy_to(fill, fill, pair_send, pair_recv.at[0], here).wait_send()


def shards(coords, eigvecs, nbr_list, nbr_count):
    f32, bf16 = jnp.float32, jnp.bfloat16
    vmem = pl.BlockSpec(memory_space=pltpu.VMEM)
    dma = pltpu.SemaphoreType.DMA

    sums = pltpu.VMEM((2 * HALF, BLOCK // 2, EIG), f32)
    return pl.pallas_call(
        kernel,
        out_shape=jax.ShapeDtypeStruct((EIG, BLOCK), f32),
        in_specs=[pl.BlockSpec(memory_space=pl.ANY)] * 3 + [pl.BlockSpec(memory_space=pltpu.SMEM)],
        out_specs=vmem,
        scratch_shapes=[
            pltpu.VMEM((PART, REP * BLOCK), f32),
            pltpu.VMEM((EIG, BLOCK), f32),
            pltpu.VMEM((REP, BLOCK), jnp.int32),
            dma((3,)),
            pltpu.VMEM((REP, PART, BLOCK), f32),
            pltpu.VMEM((2, PACK, BLOCK), f32),
            pltpu.VMEM((REP, PART, BLOCK), f32),
            pltpu.VMEM((REP, 1, BLOCK), jnp.int32),
            pltpu.VMEM((REP, 1, BLOCK), jnp.int32),
            pltpu.VMEM((Z, 2, PACK, BLOCK), f32),
            pltpu.VMEM((PLANE, 2, PANEL, BLOCK), f32),
            pltpu.VMEM((HALF, 2, BLOCK, 4 * FEAT), bf16),
            pltpu.VMEM((4 * FEAT, WIDE), bf16),
            pltpu.VMEM((WIDE, 2 * EIG), bf16),
            pltpu.VMEM((HALF, 2, 1, BLOCK), jnp.int32),
            pltpu.VMEM((HALF, 2, 1, WIDE), f32),
            pltpu.VMEM((HALF, 2 * BLOCK, EIG), f32),
            sums, sums, sums, sums,
            dma, dma, dma, dma,
            dma, dma((2 * HALF * PIECES,)),
            dma, dma((40,)),
            dma, dma((COLS,)),
            dma, dma((2 * HALF,)),
            dma, dma((2 * HALF,)),
            dma, dma,
        ],
        compiler_params=pltpu.CompilerParams(collective_id=0, has_side_effects=True),
    )(coords, eigvecs, nbr_list, nbr_count)


def solution(mesh):
    return jax.shard_map(
        shards,
        mesh=mesh,
        in_specs=(P("rep", "blk"), P(None, ("blk", "rep")), P("blk", None), P("blk")),
        out_specs=P(None, ("blk", "rep")),
        check_vma=False,
    )
```
